256 devices in a mesh: dp: 8 (over z), seq: 32 (over y, x, core).
Axes of the slice: x: 4, y: 4, z: 8, core: 2. Of those that a mesh axis runs over, the one named last changes fastest.
Arguments:
- latents: bfloat16 [64, 2048, 64], P('dp', 'seq'), may hold values from -6 to 6
- target: bfloat16 [64, 2048, 1024], P('dp', 'seq'), may hold values from -6 to 6
- lengths: int32 [64], replicated, may hold values from 1 to 2048, 81920 in all
- in_weight: bfloat16 [3, 64, 2048], replicated, may hold values from -0.4375 to 0.4375
- in_bias: float32 [2048], replicated, may hold values from -3 to 3
- snake_alpha: float32 [2048], replicated, may hold values from 0.5 to 4
- out_weight: bfloat16 [3, 2048, 1024], replicated, may hold values from -0.078125 to 0.078125
Outputs:
- latent_grad: float32 [64, 2048, 64], P('dp', 'seq')
- clip_loss: float32 [64], P('dp')
- batch_loss: float32 [], replicated
The draws below stay inside these ranges and needn't reach their ends.
Inputs may be any that keep to these rules, and one draw needn't show every extreme that they name: `lengths`: some clip has all 2048 frames live.
All inputs are finite; a program needn't handle non-finite values.
Results may differ from the reference program's by a relative error of at most 0.0022.
Values may be sent and summed in bfloat16 or wider, within the bound.
A program may use at most 64 MiB of HBM per device.

```python
import math
import jax
import jax.numpy as jnp
import numpy as np
from jax import lax

LAT = 64
CH = 2048
OUT = 1024
FRAMES = 2048
CLIPS = 64


def shard_levels(stream_key, shape, pieces, smallest, top_value):
    def one(position, parts):
        steps = jax.random.uniform(jax.random.fold_in(jax.random.fold_in(stream_key, 6), position), (parts,), jnp.float32, smallest / len(pieces), top_value / len(pieces))
        return jnp.repeat(jnp.exp(steps), shape[position] // parts).reshape((-1,) + (1,) * (len(shape) - position - 1))

    loudness = one(*pieces[0])
    for cut in pieces[1:]:
        loudness = loudness * one(*cut)
    return loudness


def length_profile(number_of, total, most, lean):
    loads = [(1 << 20) // math.isqrt(standing ** lean) + 1 for standing in range(2, number_of + 1)]
    spare, given = total - most - (number_of - 1), [1] * (number_of - 1)
    while spare > 0:
        free = [i for i in range(number_of - 1) if given[i] < most]
        mass, left = sum([loads[i] for i in free]), spare
        for i in free:
            addition = min(most - given[i], max(1, left * loads[i] // mass), spare)
            given[i] = given[i] + addition
            spare = spare - addition
    return np.array([most] + given)


def uneven_parts(own_key, amount, total, bound, lean):
    if amount == 2:
        one = jax.random.randint(own_key, (), max(1, total - bound), min(bound, total - 1) + 1)
        return jnp.stack([one, total - one])
    tallies = jnp.asarray(length_profile(amount, total, bound, lean), jnp.int32)
    pairs = (amount - 1) // 2
    source_of, taker = tallies[1:1 + 2 * pairs:2], tallies[2:2 + 2 * pairs:2]
    room = jnp.minimum(source_of - 1, bound - taker)
    moved = jax.random.randint(jax.random.fold_in(own_key, 1), (pairs,), 0, 1 << 20) % (room + 1)
    tallies = tallies.at[1:1 + 2 * pairs:2].set(source_of - moved).at[2:2 + 2 * pairs:2].set(taker + moved)
    return tallies[jax.random.permutation(jax.random.fold_in(own_key, 2), amount)]


def gaussian(key, shape, scale, limit, pieces=(), kind=jnp.bfloat16):
    factor_of = shard_levels(key, shape, pieces, -0.22, 0.18) if pieces else 1.0
    array = jax.random.normal(key, shape, jnp.float32) * scale * factor_of
    return jnp.minimum(jnp.maximum(array, -limit), limit).astype(kind)


def setup_inputs(seed: int = 0) -> dict:
    streams_of = jax.random.split(jax.random.key(seed), 8)
    return {
        "latents": gaussian(streams_of[0], (CLIPS, FRAMES, LAT), 1.0, 6.0, ((0, 8), (1, 32))),
        "target": gaussian(streams_of[1], (CLIPS, FRAMES, OUT), 1.0, 6.0, ((0, 8), (1, 32))),
        "lengths": uneven_parts(streams_of[2], CLIPS, CLIPS * FRAMES * 5 // 8, FRAMES, 2).astype(jnp.int32),
        "in_weight": gaussian(streams_of[3], (3, LAT, CH), (3 * LAT) ** -0.5, 0.4375),
        "in_bias": gaussian(streams_of[4], (CH,), 0.5, 3.0, (), jnp.float32),
        "snake_alpha": jnp.clip(jnp.exp(jax.random.uniform(streams_of[5], (CH,), jnp.float32, math.log(0.5), math.log(4.0))), 0.5, 4.0),
        "out_weight": gaussian(streams_of[6], (3, CH, OUT), (3 * CH) ** -0.5, 0.078125),
    }


def taps_fwd(x, weight, count):
    padded = jnp.pad(x, ((1, 1), (0, 0)))
    total = jnp.dot(padded[0:count], weight[0], preferred_element_type=jnp.float32)
    total = total + jnp.dot(padded[1:count + 1], weight[1], preferred_element_type=jnp.float32)
    return total + jnp.dot(padded[2:count + 2], weight[2], preferred_element_type=jnp.float32)


def taps_back(g, weight, count):
    padded = jnp.pad(g, ((1, 1), (0, 0)))
    total = jnp.dot(padded[2:count + 2], weight[0].T, preferred_element_type=jnp.float32)
    total = total + jnp.dot(padded[1:count + 1], weight[1].T, preferred_element_type=jnp.float32)
    return total + jnp.dot(padded[0:count], weight[2].T, preferred_element_type=jnp.float32)


def reference(latents, target, lengths, in_weight, in_bias, snake_alpha, out_weight):
    frame_count = latents.shape[1]
    out_count = target.shape[2]

    def one_clip(items):
        latent, goal, length = items
        hidden = taps_fwd(latent, in_weight, frame_count) + in_bias
        act = (hidden + jnp.sin(snake_alpha * hidden) ** 2 / snake_alpha).astype(jnp.bfloat16)
        decoded = taps_fwd(act, out_weight, frame_count)
        live = jnp.arange(frame_count, dtype=jnp.int32) < length
        error = jnp.where(live[:, None], decoded - goal.astype(jnp.float32), jnp.float32(0.0))
        loss = jnp.sum(error * error) / (jnp.float32(out_count) * length.astype(jnp.float32))
        act_grad = taps_back(error.astype(jnp.bfloat16), out_weight, frame_count)
        hid_grad = (act_grad * (1.0 + jnp.sin(2.0 * snake_alpha * hidden))).astype(jnp.bfloat16)
        return taps_back(hid_grad, in_weight, frame_count), loss

    latent_grad, clip_loss = lax.map(one_clip, (latents, target, lengths))
    return latent_grad, clip_loss, jnp.mean(clip_loss)
```

```python
import numpy as np
import jax
import jax.numpy as jnp
from jax import lax
from jax.experimental import pallas as pl
from jax.experimental.pallas import tpu as pltpu
from jax.sharding import PartitionSpec as P

MESH = pl.DeviceIdType.MESH
F32 = jnp.float32
BF16 = jnp.bfloat16
WIDE = 4
GOAL = 2
NEAR = 8
TILE = 256


def fit_even(fn, terms, low, high):
    nodes = np.cos((np.arange(64) + 0.5) * np.pi / 64)
    v = 0.5 * (high + low) + 0.5 * (high - low) * nodes
    poly = np.polynomial.chebyshev.Chebyshev.fit(v, fn(v), terms - 1, domain=[low, high])
    return [float(c) for c in poly.convert(kind=np.polynomial.Polynomial).coef]


SIN_COEF = fit_even(lambda v: np.pi * np.sinc(np.sqrt(v)), 5, 0.0, 0.25)
COS_COEF = fit_even(lambda v: np.cos(np.pi * np.sqrt(v)), 6, 0.0, 0.25)


def horner(coef, v):
    total = jnp.full_like(v, coef[-1])
    for c in coef[-2::-1]:
        total = total * v + F32(c)
    return total


def dot(a, b):
    return lax.dot_general(a, b, (((1,), (0,)), ((), ())), preferred_element_type=F32)


def dot_t(a, b):
    return lax.dot_general(a, b, (((1,), (1,)), ((), ())), preferred_element_type=F32)


def make_kernel(dp_count, seq_count, clips, slab, lat, ch, out):
    far = seq_count // NEAR
    hid_rows = (slab + 6) * clips
    dec_rows = (slab + 4) * clips
    grad_rows = (slab + 2) * clips
    rows = slab * clips
    frames = slab * seq_count

    def kernel(lat_ref, goal_ref, lens_ref, win_ref, bias_ref, alpha_ref, wout_hbm,
               grad_ref, loss_ref, mean_ref,
               w, act, gain, err, gacc, sums, send_a, send_b, send_c, got_a, got_b, got_c,
               w_sem, sa, ra, sb, rb, sc, rc):
        dp = lax.axis_index("dp")
        seq = lax.axis_index("seq")
        row, col = seq // NEAR, seq % NEAR
        near = [(dp, row * NEAR + lax.rem(col + j, NEAR)) for j in range(1, NEAR)]
        over = [(dp, lax.rem(row + j, far) * NEAR + col) for j in range(1, far)]
        deep = [(lax.rem(dp + j, dp_count), seq) for j in range(1, dp_count)]

        barrier = pltpu.get_barrier_semaphore()
        for where in near + over + deep:
            pl.semaphore_signal(barrier, inc=1, device_id=where, device_id_type=MESH)

        loads = [
            pltpu.make_async_copy(wout_hbm.at[pl.ds(k * ch, ch)], w.at[pl.ds(k * ch, ch)], w_sem.at[k])
            for k in range(3)
        ]
        for load in loads:
            load.start()

        def copies(buf, slots, s_sem, r_sem, partners):
            return [
                pltpu.make_async_remote_copy(
                    src_ref=buf, dst_ref=slots.at[j], send_sem=s_sem.at[j], recv_sem=r_sem.at[j],
                    device_id=where, device_id_type=MESH,
                )
                for j, where in enumerate(partners)
            ]

        copy_a = copies(send_a, got_a, sa, ra, near)
        copy_b = copies(send_b, got_b, sb, rb, over)
        copy_c = copies(send_c, got_c, sc, rc, deep)

        first = seq * slab

        def inside(count, offset):
            pos = first + offset + lax.broadcasted_iota(jnp.int32, (count * clips, 1), 0) // clips
            return (pos >= 0) & (pos < frames)

        top, bottom = inside(3, -3), inside(3, slab)
        upper, lower = inside(1, -1), inside(1, slab)

        def forward(i, _):
            cols = pl.ds(pl.multiple_of(i * TILE, TILE), TILE)
            hidden = dot(lat_ref[...], win_ref[:, cols]) + bias_ref[:, cols]
            alpha = alpha_ref[:, cols]
            turns = hidden * (alpha * F32(1.0 / np.pi))
            r = turns - jnp.round(turns)
            v = r * r
            s = r * horner(SIN_COEF, v)
            c = horner(COS_COEF, v)
            a = hidden + (s * s) * (F32(1.0) / alpha)
            edge = 3 * clips
            a = jnp.concatenate([
                jnp.where(top, a[:edge], F32(0.0)),
                a[edge : hid_rows - edge],
                jnp.where(bottom, a[hid_rows - edge :], F32(0.0)),
            ], axis=0)
            for k in range(3):
                wide = pl.ds(pl.multiple_of(k * ch + i * TILE, TILE), TILE)
                act[:, wide] = a[k * clips : k * clips + dec_rows].astype(BF16)
            sc2 = s[2 * clips : 2 * clips + grad_rows] * c[2 * clips : 2 * clips + grad_rows]
            gain[:, cols] = F32(1.0) + F32(2.0) * sc2
            return 0

        lax.fori_loop(0, ch // TILE, forward, 0)

        for load in loads:
            load.wait()

        pos = first - GOAL + lax.broadcasted_iota(jnp.int32, (dec_rows, 1), 0) // clips
        lens = lens_ref[...]
        live = (pos >= 0) & (pos < jnp.concatenate([lens] * (slab + 4), axis=0))
        sums[...] = jnp.zeros_like(sums)

        def decode(i, _):
            cols = pl.ds(pl.multiple_of(i * TILE, TILE), TILE)
            decoded = dot(act[...], w[:, cols])
            e = jnp.where(live, decoded - goal_ref[:, cols].astype(F32), F32(0.0))
            own = e[2 * clips : 2 * clips + rows]
            sq = jnp.sum((own * own).reshape(slab, clips, TILE), axis=0)
            part = sq[:, 0:128]
            for q in range(1, TILE // 128):
                part = part + sq[:, q * 128 : (q + 1) * 128]
            sums[...] += part
            for k in range(3):
                err[k, :, cols] = e[(2 - k) * clips : (2 - k) * clips + grad_rows].astype(BF16)
            return 0

        lax.fori_loop(0, out // TILE, decode, 0)
        send_a[...] = sums[...]
        pl.semaphore_wait(barrier, len(near) + len(over) + len(deep))
        gacc[...] = jnp.zeros_like(gacc)
        size = jnp.float32(out) * lens.astype(F32)

        def backward(i, _):
            base = pl.multiple_of(i * TILE, TILE)
            cols = pl.ds(base, TILE)
            g = dot_t(err[0], w[pl.ds(base, TILE), :])
            for k in range(1, 3):
                g = g + dot_t(err[k], w[pl.ds(pl.multiple_of(k * ch + i * TILE, TILE), TILE), :])
            h = g * gain[:, cols]
            h = jnp.concatenate([
                jnp.where(upper, h[:clips], F32(0.0)),
                h[clips : grad_rows - clips],
                jnp.where(lower, h[grad_rows - clips :], F32(0.0)),
            ], axis=0)
            gacc[...] += dot_t(h.astype(BF16), win_ref[:, cols])

            @pl.when(i == 0)
            def _():
                for copy in copy_a:
                    copy.start()

            @pl.when(i == 2)
            def _():
                for copy in copy_a:
                    copy.wait()
                total = send_a[...]
                for j in range(NEAR - 1):
                    total = total + got_a[j]
                send_b[...] = total

            @pl.when(i == 3)
            def _():
                for copy in copy_b:
                    copy.start()

            @pl.when(i == 5)
            def _():
                for copy in copy_b:
                    copy.wait()
                total = send_b[...]
                for j in range(far - 1):
                    total = total + got_b[j]
                loss = jnp.sum(total, axis=1, keepdims=True) / size
                loss_ref[...] = jnp.broadcast_to(loss, loss_ref.shape)
                send_c[...] = jnp.broadcast_to(jnp.sum(loss, axis=0, keepdims=True), send_c.shape)
                for copy in copy_c:
                    copy.start()

            return 0

        lax.fori_loop(0, ch // TILE, backward, 0)
        g = gacc[...]
        grad_ref[...] = (
            g[2 * clips : 2 * clips + rows, 0:lat]
            + g[clips : clips + rows, lat : 2 * lat]
            + g[0:rows, 2 * lat : 3 * lat]
        )
        for copy in copy_c:
            copy.wait()
        total = send_c[...]
        for j in range(dp_count - 1):
            total = total + got_c[j]
        mean_ref[...] = total * F32(1.0 / (clips * dp_count))

    def vmem():
        return pl.BlockSpec(memory_space=pltpu.VMEM)

    dma = pltpu.SemaphoreType.DMA
    return pl.pallas_call(
        kernel,
        name="decoder_loss_grad",
        out_shape=(
            jax.ShapeDtypeStruct((rows, lat), F32),
            jax.ShapeDtypeStruct((clips, 128), F32),
            jax.ShapeDtypeStruct((clips, 128), F32),
        ),
        in_specs=[vmem()] * 6 + [pl.BlockSpec(memory_space=pl.ANY)],
        out_specs=(vmem(), vmem(), vmem()),
        scratch_shapes=[
            pltpu.VMEM((3 * ch, out), BF16),
            pltpu.VMEM((dec_rows, 3 * ch), BF16),
            pltpu.VMEM((grad_rows, ch), F32),
            pltpu.VMEM((3, grad_rows, out), BF16),
            pltpu.VMEM((grad_rows, 3 * lat), F32),
            pltpu.VMEM((clips, 128), F32),
            pltpu.VMEM((clips, 128), F32),
            pltpu.VMEM((clips, 128), F32),
            pltpu.VMEM((clips, 128), F32),
            pltpu.VMEM((NEAR - 1, clips, 128), F32),
            pltpu.VMEM((far - 1, clips, 128), F32),
            pltpu.VMEM((dp_count - 1, clips, 128), F32),
            dma((3,)),
            dma((NEAR - 1,)), dma((NEAR - 1,)),
            dma((far - 1,)), dma((far - 1,)),
            dma((dp_count - 1,)), dma((dp_count - 1,)),
        ],
        compiler_params=pltpu.CompilerParams(
            collective_id=0, has_side_effects=True, vmem_limit_bytes=60 * 1024 * 1024
        ),
    )


def with_halo(array, width):
    devices = lax.axis_size("seq")
    up = [(i, i + 1) for i in range(devices - 1)]
    down = [(j, i) for i, j in up]
    before = lax.ppermute(array[-width:], "seq", up)
    after = lax.ppermute(array[:width], "seq", down)
    return jnp.concatenate([before, array, after], axis=0)


def on_device(latents, target, lengths, in_weight, in_bias, snake_alpha, out_weight):
    clips, slab, lat = latents.shape
    out = target.shape[2]
    ch = in_weight.shape[2]
    lens = lax.dynamic_slice_in_dim(lengths, lax.axis_index("dp") * clips, clips)[:, None]
    wide = with_halo(jnp.swapaxes(latents, 0, 1), WIDE)
    taps = jnp.concatenate([wide[k : k + slab + 6] for k in range(3)], axis=2)
    goal = with_halo(jnp.swapaxes(target, 0, 1), GOAL)
    run = make_kernel(lax.axis_size("dp"), lax.axis_size("seq"), clips, slab, lat, ch, out)
    grad, loss, mean = run(
        taps.reshape((slab + 6) * clips, 3 * lat),
        goal.reshape((slab + 4) * clips, out),
        lens,
        in_weight.reshape(3 * lat, ch),
        in_bias[None, :],
        snake_alpha[None, :],
        out_weight.reshape(3 * ch, out),
    )
    grad = jnp.swapaxes(grad.reshape(slab, clips, lat), 0, 1)
    return (grad, loss[:, 0], mean[0, 0])


def solution(mesh):
    placed = (P("dp", "seq", None), P("dp", "seq", None), P(), P(), P(), P(), P())
    return jax.shard_map(
        on_device,
        mesh=mesh,
        in_specs=placed,
        out_specs=(P("dp", "seq", None), P("dp"), P()),
        check_vma=False,
    )
```

```python
import numpy as np
import jax
import jax.numpy as jnp
from jax import lax
from jax.experimental import pallas as pl
from jax.experimental.pallas import tpu as pltpu
from jax.sharding import PartitionSpec as P

MESH = pl.DeviceIdType.MESH
F32 = jnp.float32
BF16 = jnp.bfloat16
WIDE = 4
GOAL = 2
NEAR = 8
TILE = 256
PARTS = 24


def fit_even(fn, terms, low, high):
    nodes = np.cos((np.arange(64) + 0.5) * np.pi / 64)
    v = 0.5 * (high + low) + 0.5 * (high - low) * nodes
    poly = np.polynomial.chebyshev.Chebyshev.fit(v, fn(v), terms - 1, domain=[low, high])
    return [float(c) for c in poly.convert(kind=np.polynomial.Polynomial).coef]


SIN_COEF = fit_even(lambda v: np.pi * np.sinc(np.sqrt(v)), 5, 0.0, 0.25)
COS_COEF = fit_even(lambda v: np.cos(np.pi * np.sqrt(v)), 6, 0.0, 0.25)


def horner(coef, v):
    total = jnp.full_like(v, coef[-1])
    for c in coef[-2::-1]:
        total = total * v + F32(c)
    return total


def dot(a, b):
    return lax.dot_general(a, b, (((1,), (0,)), ((), ())), preferred_element_type=F32)


def dot_t(a, b):
    return lax.dot_general(a, b, (((1,), (1,)), ((), ())), preferred_element_type=F32)


def make_kernel(dp_count, seq_count, clips, slab, lat, ch, out):
    far = seq_count // NEAR
    hid_rows = (slab + 6) * clips
    dec_rows = (slab + 4) * clips
    grad_rows = (slab + 2) * clips
    rows = slab * clips
    part_rows = 3 * ch // PARTS
    frames = slab * seq_count

    lat_edge, goal_edge = WIDE * clips, GOAL * clips

    def kernel(lat_in, goal_in, lens_ref, win_ref, bias_ref, alpha_ref, wout_hbm,
               grad_ref, loss_ref, mean_ref,
               lat_ext, lat_ref, goal_ref, gout, w, act, gain, err, gacc, sums, send_a, send_b, send_c, got_a, got_b, got_c,
               w_sem, own_sem, hs, hr, sa, ra, sb, rb, sc, rc):
        dp = lax.axis_index("dp")
        seq = lax.axis_index("seq")
        row, col = seq // NEAR, seq % NEAR
        near = [(dp, row * NEAR + lax.rem(col + j, NEAR)) for j in range(1, NEAR)]
        over = [(dp, lax.rem(row + j, far) * NEAR + col) for j in range(1, far)]
        deep = [(lax.rem(dp + j, dp_count), seq) for j in range(1, dp_count)]

        after = (dp, lax.rem(seq + 1, seq_count))
        before = (dp, lax.rem(seq + seq_count - 1, seq_count))

        barrier = pltpu.get_barrier_semaphore()
        for where in near + over + deep + [after, before]:
            pl.semaphore_signal(barrier, inc=1, device_id=where, device_id_type=MESH)

        loads = [
            pltpu.make_async_copy(
                wout_hbm.at[pl.ds(k * part_rows, part_rows)], w.at[pl.ds(k * part_rows, part_rows)], w_sem.at[k]
            )
            for k in range(PARTS)
        ]
        own_lat = pltpu.make_async_copy(lat_in, lat_ext.at[pl.ds(lat_edge, rows)], own_sem.at[0])
        own_goal = pltpu.make_async_copy(goal_in, goal_ref.at[pl.ds(goal_edge, rows)], own_sem.at[1])
        own_lat.start()
        own_goal.start()
        for load in loads:
            load.start()
        pl.semaphore_wait(barrier, len(near) + len(over) + len(deep) + 2)

        def edge_copy(src, start, dst, to, count, j, where):
            return pltpu.make_async_remote_copy(
                src_ref=src.at[pl.ds(start, count)], dst_ref=dst.at[pl.ds(to, count)],
                send_sem=hs.at[j], recv_sem=hr.at[j], device_id=where, device_id_type=MESH,
            )

        lat_halo = [
            edge_copy(lat_in, rows - lat_edge, lat_ext, 0, lat_edge, 0, after),
            edge_copy(lat_in, 0, lat_ext, lat_edge + rows, lat_edge, 1, before),
        ]
        goal_halo = [
            edge_copy(goal_in, rows - goal_edge, goal_ref, 0, goal_edge, 2, after),
            edge_copy(goal_in, 0, goal_ref, goal_edge + rows, goal_edge, 3, before),
        ]
        for copy in lat_halo + goal_halo:
            copy.start()

        def copies(buf, slots, s_sem, r_sem, partners):
            return [
                pltpu.make_async_remote_copy(
                    src_ref=buf, dst_ref=slots.at[j], send_sem=s_sem.at[j], recv_sem=r_sem.at[j],
                    device_id=where, device_id_type=MESH,
                )
                for j, where in enumerate(partners)
            ]

        copy_a = copies(send_a, got_a, sa, ra, near)
        copy_b = copies(send_b, got_b, sb, rb, over)
        copy_c = copies(send_c, got_c, sc, rc, deep)

        first = seq * slab

        def inside(count, offset):
            pos = first + offset + lax.broadcasted_iota(jnp.int32, (count * clips, 1), 0) // clips
            return (pos >= 0) & (pos < frames)

        top, bottom = inside(3, -3), inside(3, slab)
        upper, lower = inside(1, -1), inside(1, slab)

        own_lat.wait()
        for copy in lat_halo:
            copy.wait()
        wide = lat_ext[...].astype(F32)
        wide = jnp.concatenate([
            jnp.where(seq > 0, wide[:lat_edge], F32(0.0)),
            wide[lat_edge : lat_edge + rows],
            jnp.where(seq < seq_count - 1, wide[lat_edge + rows :], F32(0.0)),
        ], axis=0)
        lat_ref[...] = jnp.concatenate(
            [wide[k * clips : k * clips + hid_rows] for k in range(3)], axis=1
        ).astype(BF16)

        def forward(i, _):
            cols = pl.ds(pl.multiple_of(i * TILE, TILE), TILE)
            hidden = dot(lat_ref[...], win_ref[:, cols]) + bias_ref[:, cols]
            alpha = alpha_ref[:, cols]
            turns = hidden * (alpha * F32(1.0 / np.pi))
            r = turns - jnp.round(turns)
            v = r * r
            s = r * horner(SIN_COEF, v)
            c = horner(COS_COEF, v)
            a = hidden + (s * s) * (F32(1.0) / alpha)
            edge = 3 * clips
            a = jnp.concatenate([
                jnp.where(top, a[:edge], F32(0.0)),
                a[edge : hid_rows - edge],
                jnp.where(bottom, a[hid_rows - edge :], F32(0.0)),
            ], axis=0)
            for k in range(3):
                wide = pl.ds(pl.multiple_of(k * ch + i * TILE, TILE), TILE)
                act[:, wide] = a[k * clips : k * clips + dec_rows].astype(BF16)
            sc2 = s[2 * clips : 2 * clips + grad_rows] * c[2 * clips : 2 * clips + grad_rows]
            gain[:, cols] = F32(1.0) + F32(2.0) * sc2
            return 0

        lax.fori_loop(0, ch // TILE, forward, 0)

        for load in loads:
            load.wait()
        own_goal.wait()
        for copy in goal_halo:
            copy.wait()

        pos = first - GOAL + lax.broadcasted_iota(jnp.int32, (dec_rows, 1), 0) // clips
        lens = lens_ref[...]
        live = (pos >= 0) & (pos < jnp.concatenate([lens] * (slab + 4), axis=0))
        sums[...] = jnp.zeros_like(sums)

        def decode(i, _):
            cols = pl.ds(pl.multiple_of(i * TILE, TILE), TILE)
            decoded = dot(act[...], w[:, cols])
            e = jnp.where(live, decoded - goal_ref[:, cols].astype(F32), F32(0.0))
            own = e[2 * clips : 2 * clips + rows]
            sq = jnp.sum((own * own).reshape(slab, clips, TILE), axis=0)
            part = sq[:, 0:128]
            for q in range(1, TILE // 128):
                part = part + sq[:, q * 128 : (q + 1) * 128]
            sums[...] += part
            for k in range(3):
                err[k, :, cols] = e[(2 - k) * clips : (2 - k) * clips + grad_rows].astype(BF16)
            return 0

        lax.fori_loop(0, out // TILE, decode, 0)
        send_a[...] = sums[...]
        gacc[...] = jnp.zeros_like(gacc)
        for copy in copy_a:
            copy.start()
        size = jnp.float32(out) * lens.astype(F32)

        def backward(i, _):
            base = pl.multiple_of(i * TILE, TILE)
            cols = pl.ds(base, TILE)
            g = dot_t(err[0], w[pl.ds(base, TILE), :])
            for k in range(1, 3):
                g = g + dot_t(err[k], w[pl.ds(pl.multiple_of(k * ch + i * TILE, TILE), TILE), :])
            h = g * gain[:, cols]
            h = jnp.concatenate([
                jnp.where(upper, h[:clips], F32(0.0)),
                h[clips : grad_rows - clips],
                jnp.where(lower, h[grad_rows - clips :], F32(0.0)),
            ], axis=0)
            gacc[...] += dot_t(h.astype(BF16), win_ref[:, cols])

            @pl.when(i == 1)
            def _():
                for copy in copy_a:
                    copy.wait()
                total = send_a[...]
                for j in range(NEAR - 1):
                    total = total + got_a[j]
                send_b[...] = total

            @pl.when(i == 2)
            def _():
                for copy in copy_b:
                    copy.start()

            @pl.when(i == 4)
            def _():
                for copy in copy_b:
                    copy.wait()
                total = send_b[...]
                for j in range(far - 1):
                    total = total + got_b[j]
                loss = jnp.sum(total, axis=1, keepdims=True) / size
                loss_ref[...] = jnp.broadcast_to(loss, loss_ref.shape)
                send_c[...] = jnp.broadcast_to(jnp.sum(loss, axis=0, keepdims=True), send_c.shape)

            @pl.when(i == 5)
            def _():
                for copy in copy_c:
                    copy.start()

            return 0

        lax.fori_loop(0, ch // TILE, backward, 0)
        g = gacc[...]
        gout[:, 0:lat] = (
            g[2 * clips : 2 * clips + rows, 0:lat]
            + g[clips : clips + rows, lat : 2 * lat]
            + g[0:rows, 2 * lat : 3 * lat]
        )
        for c in range(clips):
            grad_ref[c] = gout[pl.ds(c, slab, stride=clips), :][:, 0:lat]
        for copy in copy_c:
            copy.wait()
        total = send_c[...]
        for j in range(dp_count - 1):
            total = total + got_c[j]
        mean_ref[...] = total * F32(1.0 / (clips * dp_count))

    def vmem():
        return pl.BlockSpec(memory_space=pltpu.VMEM)

    dma = pltpu.SemaphoreType.DMA
    return pl.pallas_call(
        kernel,
        name="decoder_loss_grad",
        out_shape=(
            jax.ShapeDtypeStruct((clips, slab, lat), F32),
            jax.ShapeDtypeStruct((clips, 128), F32),
            jax.ShapeDtypeStruct((clips, 128), F32),
        ),
        in_specs=[pl.BlockSpec(memory_space=pl.ANY)] * 2 + [vmem()] * 4
        + [pl.BlockSpec(memory_space=pl.ANY)],
        out_specs=(vmem(), vmem(), vmem()),
        scratch_shapes=[
            pltpu.VMEM((rows + 2 * lat_edge, lat), BF16),
            pltpu.VMEM((hid_rows, 3 * lat), BF16),
            pltpu.VMEM((dec_rows, out), BF16),
            pltpu.VMEM((rows, 128), F32),
            pltpu.VMEM((3 * ch, out), BF16),
            pltpu.VMEM((dec_rows, 3 * ch), BF16),
            pltpu.VMEM((grad_rows, ch), F32),
            pltpu.VMEM((3, grad_rows, out), BF16),
            pltpu.VMEM((grad_rows, 3 * lat), F32),
            pltpu.VMEM((clips, 128), F32),
            pltpu.VMEM((clips, 128), F32),
            pltpu.VMEM((clips, 128), F32),
            pltpu.VMEM((clips, 128), F32),
            pltpu.VMEM((NEAR - 1, clips, 128), F32),
            pltpu.VMEM((far - 1, clips, 128), F32),
            pltpu.VMEM((dp_count - 1, clips, 128), F32),
            dma((PARTS,)), dma((2,)), dma((4,)), dma((4,)),
            dma((NEAR - 1,)), dma((NEAR - 1,)),
            dma((far - 1,)), dma((far - 1,)),
            dma((dp_count - 1,)), dma((dp_count - 1,)),
        ],
        compiler_params=pltpu.CompilerParams(
            collective_id=0, has_side_effects=True, vmem_limit_bytes=60 * 1024 * 1024
        ),
    )


def on_device(latents, target, lengths, in_weight, in_bias, snake_alpha, out_weight):
    clips, slab, lat = latents.shape
    out = target.shape[2]
    ch = in_weight.shape[2]
    lens = lax.dynamic_slice_in_dim(lengths, lax.axis_index("dp") * clips, clips)[:, None]
    run = make_kernel(lax.axis_size("dp"), lax.axis_size("seq"), clips, slab, lat, ch, out)
    grad, loss, mean = run(
        jnp.swapaxes(latents, 0, 1).reshape(slab * clips, lat),
        jnp.swapaxes(target, 0, 1).reshape(slab * clips, out),
        lens,
        in_weight.reshape(3 * lat, ch),
        in_bias[None, :],
        snake_alpha[None, :],
        out_weight.reshape(3 * ch, out),
    )
    return (grad, loss[:, 0], mean[0, 0])


def solution(mesh):
    placed = (P("dp", "seq", None), P("dp", "seq", None), P(), P(), P(), P(), P())
    return jax.shard_map(
        on_device,
        mesh=mesh,
        in_specs=placed,
        out_specs=(P("dp", "seq", None), P("dp"), P()),
        check_vma=False,
    )
```

```python
import numpy as np
import jax
import jax.numpy as jnp
from jax import lax
from jax.experimental import pallas as pl
from jax.experimental.pallas import tpu as pltpu
from jax.sharding import PartitionSpec as P

MESH = pl.DeviceIdType.MESH
F32 = jnp.float32
BF16 = jnp.bfloat16
WIDE = 4
GOAL = 2
NEAR = 8
TILE = 256


def fit_even(fn, terms, low, high):
    nodes = np.cos((np.arange(64) + 0.5) * np.pi / 64)
    v = 0.5 * (high + low) + 0.5 * (high - low) * nodes
    poly = np.polynomial.chebyshev.Chebyshev.fit(v, fn(v), terms - 1, domain=[low, high])
    return [float(c) for c in poly.convert(kind=np.polynomial.Polynomial).coef]


SIN_COEF = fit_even(lambda v: np.pi * np.sinc(np.sqrt(v)), 5, 0.0, 0.25)
COS_COEF = fit_even(lambda v: np.cos(np.pi * np.sqrt(v)), 6, 0.0, 0.25)


def horner(coef, v):
    total = jnp.full_like(v, coef[-1])
    for c in coef[-2::-1]:
        total = total * v + F32(c)
    return total


def dot(a, b):
    return lax.dot_general(a, b, (((1,), (0,)), ((), ())), preferred_element_type=F32)


def dot_t(a, b):
    return lax.dot_general(a, b, (((1,), (1,)), ((), ())), preferred_element_type=F32)


def make_kernel(dp_count, seq_count, clips, slab, lat, ch, out):
    far = seq_count // NEAR
    hid_rows = (slab + 6) * clips
    dec_rows = (slab + 4) * clips
    grad_rows = (slab + 2) * clips
    rows = slab * clips
    steps = ch // TILE
    frames = slab * seq_count

    lat_edge, goal_edge = WIDE * clips, GOAL * clips

    def kernel(lat_in, goal_in, lens_ref, win_ref, bias_ref, alpha_ref, wout_hbm,
               grad_ref, loss_ref, mean_ref,
               lat_ext, lat_ref, goal_ref, gout, w, act_a, act_b, dec, gain, err, gacc, sums, send_a, send_b, send_c, got_a, got_b, got_c,
               w_sem, own_sem, hs, hr, sa, ra, sb, rb, sc, rc):
        dp = lax.axis_index("dp")
        seq = lax.axis_index("seq")
        row, col = seq // NEAR, seq % NEAR
        near = [(dp, row * NEAR + lax.rem(col + j, NEAR)) for j in range(1, NEAR)]
        over = [(dp, lax.rem(row + j, far) * NEAR + col) for j in range(1, far)]
        deep = [(lax.rem(dp + j, dp_count), seq) for j in range(1, dp_count)]

        after = (dp, lax.rem(seq + 1, seq_count))
        before = (dp, lax.rem(seq + seq_count - 1, seq_count))

        barrier = pltpu.get_barrier_semaphore()
        for where in near + over + deep + [after, before]:
            pl.semaphore_signal(barrier, inc=1, device_id=where, device_id_type=MESH)

        loads = [
            pltpu.make_async_copy(
                wout_hbm.at[pl.ds(k * ch + i * TILE, TILE)], w.at[pl.ds((3 * i + k) * TILE, TILE)],
                w_sem.at[3 * i + k],
            )
            for i in range(steps) for k in range(3)
        ]
        own_lat = pltpu.make_async_copy(lat_in, lat_ext.at[pl.ds(lat_edge, rows)], own_sem.at[0])
        own_goal = pltpu.make_async_copy(goal_in, goal_ref.at[pl.ds(goal_edge, rows)], own_sem.at[1])
        own_lat.start()
        own_goal.start()
        for load in loads:
            load.start()
        pl.semaphore_wait(barrier, len(near) + len(over) + len(deep) + 2)

        def edge_copy(src, start, dst, to, count, j, where):
            return pltpu.make_async_remote_copy(
                src_ref=src.at[pl.ds(start, count)], dst_ref=dst.at[pl.ds(to, count)],
                send_sem=hs.at[j], recv_sem=hr.at[j], device_id=where, device_id_type=MESH,
            )

        lat_halo = [
            edge_copy(lat_in, rows - lat_edge, lat_ext, 0, lat_edge, 0, after),
            edge_copy(lat_in, 0, lat_ext, lat_edge + rows, lat_edge, 1, before),
        ]
        goal_halo = [
            edge_copy(goal_in, rows - goal_edge, goal_ref, 0, goal_edge, 2, after),
            edge_copy(goal_in, 0, goal_ref, goal_edge + rows, goal_edge, 3, before),
        ]
        for copy in lat_halo + goal_halo:
            copy.start()

        def copies(buf, slots, s_sem, r_sem, partners):
            return [
                pltpu.make_async_remote_copy(
                    src_ref=buf, dst_ref=slots.at[j], send_sem=s_sem.at[j], recv_sem=r_sem.at[j],
                    device_id=where, device_id_type=MESH,
                )
                for j, where in enumerate(partners)
            ]

        copy_a = copies(send_a, got_a, sa, ra, near)
        copy_b = copies(send_b, got_b, sb, rb, over)
        copy_c = copies(send_c, got_c, sc, rc, deep)

        first = seq * slab

        def inside(count, offset):
            pos = first + offset + lax.broadcasted_iota(jnp.int32, (count * clips, 1), 0) // clips
            return (pos >= 0) & (pos < frames)

        top, bottom = inside(3, -3), inside(3, slab)
        upper, lower = inside(1, -1), inside(1, slab)

        own_lat.wait()
        for copy in lat_halo:
            copy.wait()
        wide = lat_ext[...].astype(F32)
        wide = jnp.concatenate([
            jnp.where(seq > 0, wide[:lat_edge], F32(0.0)),
            wide[lat_edge : lat_edge + rows],
            jnp.where(seq < seq_count - 1, wide[lat_edge + rows :], F32(0.0)),
        ], axis=0)
        lat_ref[...] = jnp.concatenate(
            [wide[k * clips : k * clips + hid_rows] for k in range(3)], axis=1
        ).astype(BF16)

        def forward(i, act):
            cols = pl.ds(pl.multiple_of(i * TILE, TILE), TILE)
            hidden = dot(lat_ref[...], win_ref[:, cols]) + bias_ref[:, cols]
            alpha = alpha_ref[:, cols]
            turns = hidden * (alpha * F32(1.0 / np.pi))
            r = turns - jnp.round(turns)
            v = r * r
            s = r * horner(SIN_COEF, v)
            c = horner(COS_COEF, v)
            a = hidden + (s * s) * (F32(1.0) / alpha)
            edge = 3 * clips
            a = jnp.concatenate([
                jnp.where(top, a[:edge], F32(0.0)),
                a[edge : hid_rows - edge],
                jnp.where(bottom, a[hid_rows - edge :], F32(0.0)),
            ], axis=0)
            for k in range(3):
                act[:, k * TILE : (k + 1) * TILE] = a[k * clips : k * clips + dec_rows].astype(BF16)
            sc2 = s[2 * clips : 2 * clips + grad_rows] * c[2 * clips : 2 * clips + grad_rows]
            gain[:, cols] = F32(1.0) + F32(2.0) * sc2

        def arrived(i):
            for k in range(3):
                pltpu.make_async_copy(
                    wout_hbm.at[pl.ds(pl.multiple_of(k * ch + i * TILE, TILE), TILE)],
                    w.at[pl.ds(pl.multiple_of((3 * i + k) * TILE, TILE), TILE)],
                    w_sem.at[3 * i + k],
                ).wait()

        def decode_part(i, act):
            span = pl.ds(pl.multiple_of(3 * i * TILE, TILE), 3 * TILE)
            for n in range(out // TILE):
                dec[:, n * TILE : (n + 1) * TILE] += dot(act[...], w[span, n * TILE : (n + 1) * TILE])

        dec[...] = jnp.zeros_like(dec)
        forward(0, act_a)

        def pair(j, _):
            arrived(2 * j)
            forward(2 * j + 1, act_b)
            decode_part(2 * j, act_a)
            arrived(2 * j + 1)
            forward(2 * j + 2, act_a)
            decode_part(2 * j + 1, act_b)
            return 0

        lax.fori_loop(0, steps // 2 - 1, pair, 0)
        arrived(steps - 2)
        forward(steps - 1, act_b)
        decode_part(steps - 2, act_a)
        arrived(steps - 1)
        decode_part(steps - 1, act_b)
        own_goal.wait()
        for copy in goal_halo:
            copy.wait()

        pos = first - GOAL + lax.broadcasted_iota(jnp.int32, (dec_rows, 1), 0) // clips
        clip = lax.broadcasted_iota(jnp.int32, (clips, 1), 0)
        lens = jnp.zeros((clips, 1), jnp.int32)
        for c in range(clips):
            lens = jnp.where(clip == c, lens_ref[dp * clips + c], lens)
        live = (pos >= 0) & (pos < jnp.concatenate([lens] * (slab + 4), axis=0))
        sums[...] = jnp.zeros_like(sums)

        def decode(i, _):
            cols = pl.ds(pl.multiple_of(i * TILE, TILE), TILE)
            e = jnp.where(live, dec[:, cols] - goal_ref[:, cols].astype(F32), F32(0.0))
            own = e[2 * clips : 2 * clips + rows]
            sq = jnp.sum((own * own).reshape(slab, clips, TILE), axis=0)
            part = sq[:, 0:128]
            for q in range(1, TILE // 128):
                part = part + sq[:, q * 128 : (q + 1) * 128]
            sums[...] += part
            for k in range(3):
                err[k, :, cols] = e[(2 - k) * clips : (2 - k) * clips + grad_rows].astype(BF16)
            return 0

        lax.fori_loop(0, out // TILE, decode, 0)
        send_a[...] = sums[...]
        gacc[...] = jnp.zeros_like(gacc)
        for copy in copy_a:
            copy.start()
        size = jnp.float32(out) * lens.astype(F32)

        def backward(i, _):
            cols = pl.ds(pl.multiple_of(i * TILE, TILE), TILE)
            g = dot_t(err[0], w[pl.ds(pl.multiple_of(3 * i * TILE, TILE), TILE), :])
            for k in range(1, 3):
                g = g + dot_t(err[k], w[pl.ds(pl.multiple_of((3 * i + k) * TILE, TILE), TILE), :])
            h = g * gain[:, cols]
            h = jnp.concatenate([
                jnp.where(upper, h[:clips], F32(0.0)),
                h[clips : grad_rows - clips],
                jnp.where(lower, h[grad_rows - clips :], F32(0.0)),
            ], axis=0)
            gacc[...] += dot_t(h.astype(BF16), win_ref[:, cols])

            @pl.when(i == 1)
            def _():
                for copy in copy_a:
                    copy.wait()
                total = send_a[...]
                for j in range(NEAR - 1):
                    total = total + got_a[j]
                send_b[...] = total

            @pl.when(i == 2)
            def _():
                for copy in copy_b:
                    copy.start()

            @pl.when(i == 4)
            def _():
                for copy in copy_b:
                    copy.wait()
                total = send_b[...]
                for j in range(far - 1):
                    total = total + got_b[j]
                loss = jnp.sum(total, axis=1, keepdims=True) / size
                lane = lax.broadcasted_iota(jnp.int32, (clips, 128), 1)
                spread = jnp.where(lane == clip, loss, F32(0.0))
                loss_ref[...] = jnp.sum(spread, axis=0, keepdims=True)[:, :clips]
                send_c[...] = jnp.broadcast_to(jnp.sum(loss, axis=0, keepdims=True), send_c.shape)

            @pl.when(i == 5)
            def _():
                for copy in copy_c:
                    copy.start()

            return 0

        lax.fori_loop(0, ch // TILE, backward, 0)
        g = gacc[...]
        gout[:, 0:lat] = (
            g[2 * clips : 2 * clips + rows, 0:lat]
            + g[clips : clips + rows, lat : 2 * lat]
            + g[0:rows, 2 * lat : 3 * lat]
        )
        for c in range(clips):
            grad_ref[c] = gout[pl.ds(c, slab, stride=clips), :][:, 0:lat]
        for copy in copy_c:
            copy.wait()
        total = send_c[...]
        for j in range(dp_count - 1):
            total = total + got_c[j]
        mean_ref[...] = total[0:1, 0:1] * F32(1.0 / (clips * dp_count))

    def vmem():
        return pl.BlockSpec(memory_space=pltpu.VMEM)

    dma = pltpu.SemaphoreType.DMA
    return pl.pallas_call(
        kernel,
        name="decoder_loss_grad",
        out_shape=(
            jax.ShapeDtypeStruct((clips, slab, lat), F32),
            jax.ShapeDtypeStruct((1, clips), F32),
            jax.ShapeDtypeStruct((1, 1), F32),
        ),
        in_specs=[pl.BlockSpec(memory_space=pl.ANY)] * 2 + [pl.BlockSpec(memory_space=pltpu.SMEM)] + [vmem()] * 3
        + [pl.BlockSpec(memory_space=pl.ANY)],
        out_specs=(vmem(), vmem(), vmem()),
        scratch_shapes=[
            pltpu.VMEM((rows + 2 * lat_edge, lat), BF16),
            pltpu.VMEM((hid_rows, 3 * lat), BF16),
            pltpu.VMEM((dec_rows, out), BF16),
            pltpu.VMEM((rows, 128), F32),
            pltpu.VMEM((3 * ch, out), BF16),
            pltpu.VMEM((dec_rows, 3 * TILE), BF16),
            pltpu.VMEM((dec_rows, 3 * TILE), BF16),
            pltpu.VMEM((dec_rows, out), F32),
            pltpu.VMEM((grad_rows, ch), F32),
            pltpu.VMEM((3, grad_rows, out), BF16),
            pltpu.VMEM((grad_rows, 3 * lat), F32),
            pltpu.VMEM((clips, 128), F32),
            pltpu.VMEM((clips, 128), F32),
            pltpu.VMEM((clips, 128), F32),
            pltpu.VMEM((clips, 128), F32),
            pltpu.VMEM((NEAR - 1, clips, 128), F32),
            pltpu.VMEM((far - 1, clips, 128), F32),
            pltpu.VMEM((dp_count - 1, clips, 128), F32),
            dma((3 * steps,)), dma((2,)), dma((4,)), dma((4,)),
            dma((NEAR - 1,)), dma((NEAR - 1,)),
            dma((far - 1,)), dma((far - 1,)),
            dma((dp_count - 1,)), dma((dp_count - 1,)),
        ],
        compiler_params=pltpu.CompilerParams(
            collective_id=0, has_side_effects=True, vmem_limit_bytes=60 * 1024 * 1024
        ),
    )


def on_device(latents, target, lengths, in_weight, in_bias, snake_alpha, out_weight):
    clips, slab, lat = latents.shape
    out = target.shape[2]
    ch = in_weight.shape[2]
    run = make_kernel(lax.axis_size("dp"), lax.axis_size("seq"), clips, slab, lat, ch, out)
    grad, loss, mean = run(
        jnp.swapaxes(latents, 0, 1).reshape(slab * clips, lat),
        jnp.swapaxes(target, 0, 1).reshape(slab * clips, out),
        lengths,
        in_weight.reshape(3 * lat, ch),
        in_bias[None, :],
        snake_alpha[None, :],
        out_weight.reshape(3 * ch, out),
    )
    return (grad, loss.reshape(clips), mean.reshape(()))


def solution(mesh):
    placed = (P("dp", "seq", None), P("dp", "seq", None), P(), P(), P(), P(), P())
    return jax.shard_map(
        on_device,
        mesh=mesh,
        in_specs=placed,
        out_specs=(P("dp", "seq", None), P("dp"), P()),
        check_vma=False,
    )
```
